512 devices in a mesh: dom: 16 (over x, z_hi, core), ctx: 32 (over z_lo, y).
Axes of the slice: x: 4, y: 8, z: 8 (z_hi: 2, z_lo: 4; z = z_hi * 4 + z_lo), core: 2. Of those that a mesh axis runs over, the one named last changes fastest.
Arguments:
- q_new: bfloat16 [65536, 4096], P(('dom', 'ctx')), may hold values from -40 to 40
- kv_new: bfloat16 [65536, 2, 512], P(('dom', 'ctx')), may hold values from -5 to 5
- prompt_kv: bfloat16 [2048, 2, 512], P('ctx'), may hold values from -5 to 5
- cache_kv: bfloat16 [512, 256, 2, 512], P('dom', 'ctx'), may hold values from -5 to 5
- ancestors: int32 [512], replicated, may hold values from 0 to 511, as said below
- lengths: int32 [512], replicated, may hold values from 1 to 32, as said below
Outputs:
- attended: bfloat16 [65536, 4096], P(('dom', 'ctx'))
The draws below stay inside these ranges and needn't reach their ends.
Inputs may be any that keep to these rules, and one draw needn't show every extreme that they name: The 512 particles form 16 groups of 32 consecutive ones; within a group, each run of 4 consecutive particles takes all its ancestors from one group, and the runs of a group take them from different groups (its own among the possible ones). Ancestors repeat freely. `lengths`: both ends are reached.
All inputs are finite; a program needn't handle non-finite values.
Results may differ from the reference program's by a relative error of at most 0.022.
Values may be sent and summed in bfloat16 or wider, within the bound.
A program may use at most 128 MiB of HBM per device.

```python
import jax
import jax.numpy as jnp
from jax import lax

HD = 128
H = 32
KVH = 4
SPAN = 128
PAGE = 8
GQ = 8
PG = 32
P_SIZE = 512
CAP = 4
MAXP = 32
GEN = 256
PROMPT = 2048
N_DOM = 16


def prompt_base(key):
    sub_key = jax.random.fold_in(key, 5)
    samples = jnp.clip(jax.random.normal(sub_key, (PROMPT, 2, KVH * HD), jnp.float32), -5.0, 5.0)
    return samples


def draw_prompt_kv(key, part):
    return prompt_base(key).astype(jnp.bfloat16)


def draw_q_new(key, part):
    sub_key = jax.random.fold_in(key, 6)
    samples = jnp.clip(2.5 * jax.random.normal(sub_key, (P_SIZE * SPAN, H * HD), jnp.float32), -12.5, 12.5)
    return samples.astype(jnp.bfloat16)


def draw_ancestors(key, part):
    half_groups = N_DOM // 2
    group_keys = jax.random.split(jax.random.fold_in(key, 21), N_DOM)
    orders = jax.vmap(lambda key_one: jax.random.permutation(key_one, N_DOM))(group_keys)[:, :half_groups]
    sources = jnp.repeat(orders, CAP, axis=1)
    chosen = jax.random.randint(jax.random.fold_in(key, 22), (N_DOM, PG), 0, PG)
    return (sources * PG + chosen).reshape(P_SIZE).astype(jnp.int32)


def draw_lengths(key, part):
    samples = jax.random.randint(jax.random.fold_in(key, 31), (P_SIZE,), 1, MAXP + 1)
    top_spot = jax.random.randint(jax.random.fold_in(key, 32), (), 0, P_SIZE)
    low_spot = (top_spot + 1 + jax.random.randint(jax.random.fold_in(key, 33), (), 0, P_SIZE - 1)) % P_SIZE
    samples = samples.at[top_spot].set(MAXP)
    samples = samples.at[low_spot].set(1)
    return samples.astype(jnp.int32)


def shard_levels(own_key, shape, cuts, least, top_value):
    def one(axis_at, shards_of):
        steps = jax.random.uniform(jax.random.fold_in(jax.random.fold_in(own_key, 6), axis_at), (shards_of,), jnp.float32, least / len(cuts), top_value / len(cuts))
        return jnp.repeat(jnp.exp(steps), shape[axis_at] // shards_of).reshape((-1,) + (1,) * (len(shape) - axis_at - 1))

    loudness = one(*cuts[0])
    for cut in cuts[1:]:
        loudness = loudness * one(*cut)
    return loudness


def centred(own_key, extent, scale, most, shards=(), held_as=jnp.bfloat16):
    level = shard_levels(own_key, extent, shards, -0.22, 0.18) if shards else 1.0
    drawn = jax.random.normal(own_key, extent, jnp.float32) * scale * level
    return jnp.minimum(jnp.maximum(drawn, -most), most).astype(held_as)


def setup_inputs(seed: int = 0) -> dict:
    key_list = jax.random.split(jax.random.key(seed), 7)
    q_new = draw_q_new(jax.random.fold_in(key_list[6], 71), 0)
    kv_new = centred(key_list[1], (P_SIZE * SPAN, 2, KVH * HD), 1.0, 5.0, ((0, 512),))
    prompt_kv = draw_prompt_kv(jax.random.fold_in(key_list[6], 71), 0)
    cache_kv = centred(key_list[3], (P_SIZE, GEN, 2, KVH * HD), 1.0, 5.0, ((0, 16), (1, 32)))
    ancestors = draw_ancestors(jax.random.fold_in(key_list[6], 71), 0)
    lengths = draw_lengths(jax.random.fold_in(key_list[6], 71), 0)
    return {"q_new": q_new, "kv_new": kv_new, "prompt_kv": prompt_kv, "cache_kv": cache_kv, "ancestors": ancestors, "lengths": lengths}


NEGATIVE = -1e30


def reference(q_new, kv_new, prompt_kv, cache_kv, ancestors, lengths):
    prompt_keys = prompt_kv[:, 0].astype(jnp.float32).reshape(PROMPT, KVH, HD)
    prompt_values = prompt_kv[:, 1].astype(jnp.float32).reshape(PROMPT, KVH, HD)
    positions = jnp.arange(SPAN, dtype=jnp.int32)
    causal = positions[None, :] <= positions[:, None]
    cache_positions = jnp.arange(GEN, dtype=jnp.int32)
    prompt_visible = jnp.ones((SPAN, PROMPT), dtype=jnp.bool_)

    def one_particle(particle):
        anchor = ancestors[particle]
        pages = lax.dynamic_index_in_dim(cache_kv, anchor, 0, keepdims=False).astype(jnp.float32)
        page_limit = lengths[anchor] * PAGE
        queries = lax.dynamic_slice_in_dim(q_new, particle * SPAN, SPAN, 0).astype(jnp.float32).reshape(SPAN, KVH, GQ, HD)
        fresh_kv = lax.dynamic_slice_in_dim(kv_new, particle * SPAN, SPAN, 0).astype(jnp.float32)
        key_rows = jnp.concatenate([prompt_keys, pages[:, 0].reshape(GEN, KVH, HD), fresh_kv[:, 0].reshape(SPAN, KVH, HD)], axis=0)
        value_rows = jnp.concatenate([prompt_values, pages[:, 1].reshape(GEN, KVH, HD), fresh_kv[:, 1].reshape(SPAN, KVH, HD)], axis=0)
        cache_visible = jnp.broadcast_to((cache_positions < page_limit)[None, :], (SPAN, GEN))
        visible = jnp.concatenate([prompt_visible, cache_visible, causal], axis=1)[:, None, None, :]
        scores = jnp.einsum("igjd,kgd->igjk", queries, key_rows) * (HD ** -0.5)
        scores = jnp.where(visible, scores, NEGATIVE)
        maxima = jnp.max(scores, axis=-1, keepdims=True)
        weights = jnp.where(visible, jnp.exp(scores - maxima), 0.0)
        totals = jnp.sum(weights, axis=-1)
        rounded = lax.optimization_barrier(weights.astype(jnp.bfloat16)).astype(jnp.float32)
        output = jnp.einsum("igjk,kgd->igjd", rounded, value_rows) / totals[..., None]
        return output.astype(jnp.bfloat16).reshape(SPAN, H * HD)

    result = lax.map(one_particle, jnp.arange(P_SIZE, dtype=jnp.int32))
    return result.reshape(P_SIZE * SPAN, H * HD)
```

```python
import functools

import jax
import jax.numpy as jnp
from jax import lax
from jax.experimental import pallas as pl
from jax.experimental.pallas import tpu as pltpu
from jax.sharding import PartitionSpec as P

HD = 128
H = 32
KVH = 4
SPAN = 128
PAGE = 8
GQ = 8
NDOM = 16
NCTX = 32
NY = 8
NZLO = 4
PG = 32
CAP = 4
SHARD = 64
ZBLOCK = SHARD * NZLO
KVW = KVH * HD
ROWS = 2 * PAGE
NEGATIVE = -1e30
SCALE = HD ** (-0.5) * 1.4426950408889634


def place():
    dom = lax.axis_index("dom")
    ctx = lax.axis_index("ctx")
    core = dom % 2
    z_hi = (dom // 2) % 2
    x = dom // 4
    z_lo = ctx // NY
    y = ctx % NY
    return dom, ctx, x, z_hi, core, z_lo, y


def at_z(x, core, y, z):
    z = z % (2 * NZLO)
    return {"dom": (x * 2 + z // NZLO) * 2 + core, "ctx": (z % NZLO) * NY + y}


def rcopy(src, dst, send, recv, target):
    return pltpu.make_async_remote_copy(
        src_ref=src,
        dst_ref=dst,
        send_sem=send,
        recv_sem=recv,
        device_id=target,
        device_id_type=pl.DeviceIdType.MESH,
    )


def exchange_kernel(
    anc, prompt, cache, pk, gbuf, sbuf, rbuf, tbuf,
    z_send, z_recv, r_send, r_recv, l_send, l_recv, c_send, c_recv, d_send, d_recv, p_send, p_recv,
):
    dom, ctx, x, z_hi, core, z_lo, y = place()
    z = z_hi * NZLO + z_lo
    sibling = {"dom": dom + 1 - 2 * core, "ctx": ctx}
    right = {"dom": dom, "ctx": z_lo * NY + (y + 1) % NY}
    left = {"dom": dom, "ctx": z_lo * NY + (y + NY - 1) % NY}
    far = 2 - 4 * (z % 2)
    z_targets = [at_z(x, core, y, z + 1), at_z(x, core, y, z + 7), at_z(x, core, y, z + far + 8)]

    barrier = pltpu.get_barrier_semaphore()

    def greet(target):
        pl.semaphore_signal(barrier, inc=1, device_id=target, device_id_type=pl.DeviceIdType.MESH)

    for target in (z_targets[0], z_targets[1], at_z(x, core, y, z - far + 8)):
        greet(target)

    def greet_dom(o, carry):
        greet({"dom": (dom + o) % NDOM, "ctx": ctx})
        return carry

    def greet_ctx(o, carry):
        greet({"dom": dom, "ctx": (ctx + o) % NCTX})
        return carry

    lax.fori_loop(1, NDOM, greet_dom, 0)
    lax.fori_loop(1, NCTX, greet_ctx, 0)
    pk[core, y, pl.ds(z_lo * SHARD, SHARD), :] = prompt[core]

    def pick(d, carry):
        run = 0
        for r in range(PG // CAP):
            run = jnp.where(anc[d * PG + r * CAP] // PG == dom, r, run)
        for k in range(CAP):
            local = anc[d * PG + run * CAP + k] % PG
            sbuf[d, pl.ds(k * ROWS, ROWS), :] = cache[local]
        return carry

    lax.fori_loop(0, NDOM, pick, 0)
    pl.semaphore_wait(barrier, 3 + NDOM - 1 + NCTX - 1)

    own_rows = pl.ds(z_lo * SHARD, SHARD)
    z_copies = [
        rcopy(pk.at[core, y, own_rows], pk.at[core, y, own_rows], z_send.at[i], z_recv.at[i], z_targets[i])
        for i in range(3)
    ]
    for copy in z_copies:
        copy.start()

    def dom_copy(o):
        d = (dom + o) % NDOM
        return rcopy(sbuf.at[d], rbuf.at[dom], d_send.at[o], d_recv.at[o], {"dom": d, "ctx": ctx})

    def start_dom(o, carry):
        dom_copy(o).start()
        return carry

    def wait_dom(o, carry):
        dom_copy(o).wait()
        return carry

    lax.fori_loop(1, NDOM, start_dom, 0)
    rbuf[dom] = sbuf[dom]

    def core_copy(i, yy):
        return rcopy(pk.at[core, yy], pk.at[core, yy], c_send.at[i], c_recv.at[i], sibling)

    for copy in z_copies:
        copy.wait()
    core_copies = [core_copy(0, y)]
    core_copies[0].start()
    half = ZBLOCK // 2
    rights, lefts = [], []
    for t in range(4):
        yr = (y + NY - t) % NY
        yl = (y + t) % NY
        if t > 0:
            rights[t - 1].wait_recv()
            lefts[t - 1].wait_recv()
        rrows = pl.ds(0, ZBLOCK if t < 3 else half)
        lrows = pl.ds(0 if t < 3 else half, ZBLOCK if t < 3 else half)
        rights.append(
            rcopy(pk.at[core, yr, rrows], pk.at[core, yr, rrows], r_send.at[t], r_recv.at[t], right)
        )
        lefts.append(
            rcopy(pk.at[core, yl, lrows], pk.at[core, yl, lrows], l_send.at[t], l_recv.at[t], left)
        )
        rights[t].start()
        lefts[t].start()
        if t > 0:
            for i, yy in ((2 * t - 1, yr), (2 * t, yl)):
                core_copies.append(core_copy(i, yy))
                core_copies[-1].start()
    rights[3].wait_recv()
    lefts[3].wait_recv()
    core_copies.append(core_copy(7, (y + 4) % NY))
    core_copies[-1].start()

    lax.fori_loop(1, NDOM, wait_dom, 0)

    def deal(i, carry):
        source = anc[dom * PG + i] // PG
        picked = rbuf[source, pl.ds(pl.multiple_of((i % CAP) * ROWS, ROWS), ROWS), :]
        tbuf[i] = picked
        return carry

    lax.fori_loop(0, PG, deal, 0)

    def ctx_copy(o):
        i = (ctx + o) % NCTX
        return rcopy(tbuf.at[i], gbuf.at[ctx], p_send.at[o], p_recv.at[o], {"dom": dom, "ctx": i})

    def start_ctx(o, carry):
        ctx_copy(o).start()
        return carry

    def wait_ctx(o, carry):
        ctx_copy(o).wait()
        return carry

    lax.fori_loop(1, NCTX, start_ctx, 0)
    gbuf[ctx] = tbuf[ctx]
    for t in range(4):
        rights[t].wait_send()
        lefts[t].wait_send()
    for copy in core_copies:
        copy.wait()
    lax.fori_loop(1, NCTX, wait_ctx, 0)


def exchange(anc, prompt, cache):
    vmem = pl.BlockSpec(memory_space=pltpu.VMEM)
    dma = pltpu.SemaphoreType.DMA
    return pl.pallas_call(
        exchange_kernel,
        out_shape=(
            jax.ShapeDtypeStruct((2, NY, ZBLOCK, KVW), jnp.bfloat16),
            jax.ShapeDtypeStruct((NCTX, ROWS, KVW), jnp.bfloat16),
        ),
        in_specs=[pl.BlockSpec(memory_space=pltpu.SMEM), vmem, vmem],
        out_specs=(vmem, vmem),
        scratch_shapes=[
            pltpu.VMEM((NDOM, CAP * ROWS, KVW), jnp.bfloat16),
            pltpu.VMEM((NDOM, CAP * ROWS, KVW), jnp.bfloat16),
            pltpu.VMEM((NCTX, ROWS, KVW), jnp.bfloat16),
            dma((3,)), dma((3,)), dma((4,)), dma((4,)), dma((4,)), dma((4,)),
            dma((8,)), dma((8,)), dma((NDOM,)), dma((NDOM,)), dma((NCTX,)), dma((NCTX,)),
        ],
        compiler_params=pltpu.CompilerParams(
            collective_id=0, has_side_effects=True, vmem_limit_bytes=40 * 2**20
        ),
        name="exchange",
    )(anc, prompt, cache)


BLOCK = 4 * SPAN


def queries_of(q, g, part):
    begin = g * GQ * HD + part * 4 * HD
    return jnp.concatenate(
        [q[:, pl.ds(pl.multiple_of(begin + j * HD, HD), HD)] for j in range(4)], axis=0
    )


def absorb(q, state, g, part, keys, values, visible, first):
    m_ref, l_ref, acc_ref = state
    n = keys.shape[0]
    scores = lax.dot_general(
        queries_of(q, g, part), keys, (((1,), (1,)), ((), ())), preferred_element_type=jnp.float32
    )
    if visible is not None:
        scores = jnp.where(visible, scores, NEGATIVE)
    top = jnp.max(scores, axis=1, keepdims=True)
    at = g * 2 + part
    if first:
        m_new = jnp.broadcast_to(top, (BLOCK, HD))
    else:
        m_old = m_ref[at]
        m_new = jnp.maximum(m_old, top)
    weights = jnp.concatenate(
        [jnp.exp2((scores[:, i * HD : (i + 1) * HD] - m_new) * SCALE) for i in range(n // HD)], axis=1
    )
    total = weights[:, :HD]
    for i in range(1, n // HD):
        total = total + weights[:, i * HD : (i + 1) * HD]
    added = jnp.dot(weights.astype(jnp.bfloat16), values, preferred_element_type=jnp.float32)
    if first:
        l_ref[at] = total
        acc_ref[at] = added
    else:
        factor = jnp.exp2((m_old - m_new) * SCALE)
        l_ref[at] = factor * l_ref[at] + total
        acc_ref[at] = factor * acc_ref[at] + added
    m_ref[at] = m_new


def absorb_new(q, kvn, state):
    def step(i, carry):
        g, part = i // 2, i % 2
        cols = pl.ds(pl.multiple_of(g * HD, HD), HD)
        row = lax.broadcasted_iota(jnp.int32, (BLOCK, SPAN), 0) % SPAN
        col = lax.broadcasted_iota(jnp.int32, (BLOCK, SPAN), 1)
        absorb(q, state, g, part, kvn[0, :, cols], kvn[1, :, cols], col <= row, True)
        return carry

    lax.fori_loop(0, 2 * KVH, step, 0)


def absorb_prompt(q, pk, state, blocks):
    def step(i, carry):
        g, part = i // 2, i % 2
        cols = pl.ds(pl.multiple_of(g * HD, HD), HD)
        keys = jnp.concatenate([pk[0, b, :, cols] for b in blocks], axis=0)
        values = jnp.concatenate([pk[1, b, :, cols] for b in blocks], axis=0)
        absorb(q, state, g, part, keys, values, None, False)
        return carry

    lax.fori_loop(0, 2 * KVH, step, 0)


def absorb_pages(q, gbuf, limit, state):
    def step(i, carry):
        g, part = i // 2, i % 2
        cols = pl.ds(pl.multiple_of(g * HD, HD), HD)
        pages = gbuf[:, :, cols].astype(jnp.float32)
        keys = pages[:, :PAGE].reshape(NCTX * PAGE, HD).astype(jnp.bfloat16)
        values = pages[:, PAGE:].reshape(NCTX * PAGE, HD).astype(jnp.bfloat16)
        col = lax.broadcasted_iota(jnp.int32, (BLOCK, NCTX * PAGE), 1)
        absorb(q, state, g, part, keys, values, col < limit, False)
        return carry

    lax.fori_loop(0, 2 * KVH, step, 0)


def finish(state, out):
    m_ref, l_ref, acc_ref = state

    def step(i, carry):
        result = acc_ref[i] / jnp.sum(l_ref[i], axis=1, keepdims=True)
        result = result.astype(jnp.bfloat16)
        for j in range(4):
            out[:, pl.ds(pl.multiple_of(i * 4 * HD + j * HD, HD), HD)] = result[j * SPAN : (j + 1) * SPAN]
        return carry

    lax.fori_loop(0, 2 * KVH, step, 0)


def attend_kernel(anc, lengths, q, kvn, pk, gbuf, out, m_ref, l_ref, acc_ref):
    dom, ctx = lax.axis_index("dom"), lax.axis_index("ctx")
    limit = lengths[anc[dom * PG + ctx]] * PAGE
    state = (m_ref, l_ref, acc_ref)
    absorb_new(q, kvn, state)
    for b in range(0, NY, 2):
        absorb_prompt(q, pk, state, (b, b + 1))
    absorb_pages(q, gbuf, limit, state)
    finish(state, out)


def attend(anc, lengths, q, kvn, pk, gbuf):
    vmem = pl.BlockSpec(memory_space=pltpu.VMEM)
    smem = pl.BlockSpec(memory_space=pltpu.SMEM)
    return pl.pallas_call(
        attend_kernel,
        out_shape=jax.ShapeDtypeStruct((SPAN, H * HD), jnp.bfloat16),
        in_specs=[smem, smem, vmem, vmem, vmem, vmem],
        out_specs=vmem,
        scratch_shapes=[pltpu.VMEM((2 * KVH, BLOCK, HD), jnp.float32)] * 3,
        compiler_params=pltpu.CompilerParams(vmem_limit_bytes=50 * 2**20),
        name="attend",
    )(anc, lengths, q, kvn, pk, gbuf)


def on_device(q_new, kv_new, prompt_kv, cache_kv, ancestors, lengths):
    prompt = prompt_kv.transpose(1, 0, 2)
    cache = cache_kv.transpose(0, 2, 1, 3).reshape(PG, ROWS, KVW)
    kvn = kv_new.transpose(1, 0, 2)
    pk, gbuf = exchange(ancestors, prompt, cache)
    return attend(ancestors, lengths, q_new, kvn, pk, gbuf)


def solution(mesh):
    placed = (
        P(("dom", "ctx"), None),
        P(("dom", "ctx"), None, None),
        P("ctx", None, None),
        P("dom", "ctx", None, None),
        P(),
        P(),
    )
    return jax.shard_map(
        on_device, mesh=mesh, in_specs=placed, out_specs=P(("dom", "ctx"), None), check_vma=False
    )
```

```python
import functools

import jax
import jax.numpy as jnp
from jax import lax
from jax.experimental import pallas as pl
from jax.experimental.pallas import tpu as pltpu
from jax.sharding import PartitionSpec as P

HD = 128
H = 32
KVH = 4
SPAN = 128
PAGE = 8
GQ = 8
NDOM = 16
NCTX = 32
NY = 8
NZLO = 4
PG = 32
CAP = 4
SHARD = 64
ZBLOCK = SHARD * NZLO
KVW = KVH * HD
ROWS = 2 * PAGE
RUN = CAP * ROWS
NEGATIVE = -1e30
SCALE = HD ** (-0.5) * 1.4426950408889634


def place():
    dom = lax.axis_index("dom")
    ctx = lax.axis_index("ctx")
    core = dom % 2
    z_hi = (dom // 2) % 2
    x = dom // 4
    z_lo = ctx // NY
    y = ctx % NY
    return dom, ctx, x, z_hi, core, z_lo, y


def at_z(x, core, y, z):
    z = z % (2 * NZLO)
    return {"dom": (x * 2 + z // NZLO) * 2 + core, "ctx": (z % NZLO) * NY + y}


def rcopy(src, dst, send, recv, target):
    return pltpu.make_async_remote_copy(
        src_ref=src,
        dst_ref=dst,
        send_sem=send,
        recv_sem=recv,
        device_id=target,
        device_id_type=pl.DeviceIdType.MESH,
    )


def attend_kernel(
    anc_hbm, len_hbm, prompt, cache, q_hbm, kvn, out_hbm,
    anc, lens, q, out, pk, abuf, bbuf, ybuf, gbuf, m_ref, l_ref, acc_ref,
    ar0, ar1, ar2, ar3, br0, br1, br2, br3, in_sem, z_send, z_recv, r_send, r_recv, l_send, l_recv, c_send, c_recv,
    a_send, a_recv, b_send, b_recv, p_send, p_recv, out_sem,
):
    dom, ctx, x, z_hi, core, z_lo, y = place()
    z = z_hi * NZLO + z_lo
    e = x * 2 + core
    sibling = {"dom": dom + 1 - 2 * core, "ctx": ctx}
    right = {"dom": dom, "ctx": z_lo * NY + (y + 1) % NY}
    left = {"dom": dom, "ctx": z_lo * NY + (y + NY - 1) % NY}
    state = (m_ref, l_ref, acc_ref)
    arecv, brecv = (ar0, ar1, ar2, ar3), (br0, br1, br2, br3)

    def at_e(o):
        other = (e + o) % NY
        return {"dom": ((other // 2) * 2 + z_hi) * 2 + other % 2, "ctx": ctx}

    def at_y(o):
        return {"dom": dom, "ctx": z_lo * NY + (y + o) % NY}

    barrier = pltpu.get_barrier_semaphore()
    fetch = [
        pltpu.make_async_copy(anc_hbm, anc, in_sem.at[0]),
        pltpu.make_async_copy(len_hbm, lens, in_sem.at[1]),
        pltpu.make_async_copy(q_hbm, q, in_sem.at[2]),
    ]
    for copy in fetch:
        copy.start()
    for o in range(1, NY):
        for target in (at_e(o), at_z(x, core, y, z + o), at_y(o)):
            pl.semaphore_signal(barrier, inc=1, device_id=target, device_id_type=pl.DeviceIdType.MESH)
    own_rows = pl.ds(z_lo * SHARD, SHARD)
    pk[core, y, own_rows, :] = prompt[core]
    fetch[0].wait()
    fetch[1].wait()

    def pick_first(d, carry):
        run = 0
        for r in range(PG // CAP):
            run = jnp.where(anc[d * PG + r * CAP] // PG == dom, r, run)
        for k in range(CAP):
            page = cache[anc[d * PG + run * CAP + k] % PG]
            for g in range(KVH):
                abuf[g, (d // 4) * 2 + d % 2, (d // 2) % 2, k * ROWS : (k + 1) * ROWS, :] = page[
                    :, g * HD : (g + 1) * HD
                ]
        return carry

    lax.fori_loop(0, NDOM, pick_first, 0)
    pl.semaphore_wait(barrier, 3 * (NY - 1))

    far = 2 - 4 * (z % 2)
    z_copies = [
        rcopy(pk.at[core, y, own_rows], pk.at[core, y, own_rows], z_send.at[i], z_recv.at[i],
              at_z(x, core, y, z + hop + 8))
        for i, hop in enumerate((1, -1, far))
    ]
    for copy in z_copies:
        copy.start()

    def a_copy(g, o):
        return rcopy(abuf.at[g, (e + o) % NY], arecv[g].at[e], a_send.at[g, o], a_recv.at[g, o], at_e(o))

    def b_copy(g, o):
        return rcopy(bbuf.at[g, (z + o) % NY], brecv[g].at[z], b_send.at[g, o], b_recv.at[g, o],
                     at_z(x, core, y, z + o))

    def p_copy(g, o):
        return rcopy(ybuf.at[g, (y + o) % NY], gbuf.at[g, y], p_send.at[g, o], p_recv.at[g, o], at_y(o))

    def start_all(make, g):
        for o in range(1, NY):
            make(g, o).start()

    def wait_all(make, g):
        for o in range(1, NY):
            make(g, o).wait()

    for g in range(KVH):
        start_all(a_copy, g)
        arecv[g][e] = abuf[g, e]

    def along_z(g):
        wait_all(a_copy, g)

        def pick(zz, carry):
            to_hi = zz // NZLO
            for j in range(2):
                source = anc[(x * 4 + to_hi * 2 + core) * PG + (zz % NZLO) * 8 + j * CAP] // PG
                bbuf[g, zz, j] = arecv[g][(source // 4) * 2 + source % 2, to_hi]
            return carry

        lax.fori_loop(0, NY, pick, 0)
        start_all(b_copy, g)
        brecv[g][z] = bbuf[g, z]

    def along_y(g):
        wait_all(b_copy, g)
        for j in range(2):
            source = anc[dom * PG + z_lo * 8 + j * CAP] // PG
            for zl in range(NZLO):
                pages = brecv[g][((source // 2) % 2) * NZLO + zl, j]
                for k in range(CAP):
                    ybuf[g, j * CAP + k, zl * ROWS : (zl + 1) * ROWS, :] = pages[k * ROWS : (k + 1) * ROWS]
        start_all(p_copy, g)
        gbuf[g, y] = ybuf[g, y]

    def core_copy(i, yy):
        return rcopy(pk.at[core, yy], pk.at[core, yy], c_send.at[i], c_recv.at[i], sibling)

    half = ZBLOCK // 2
    rights, lefts, cores = [], [], []

    def ring_step(t):
        yr = (y + NY - t) % NY
        yl = (y + t) % NY
        if t == 0:
            for copy in z_copies:
                copy.wait()
        else:
            rights[t - 1].wait_recv()
            lefts[t - 1].wait_recv()
        if t < 4:
            rrows = pl.ds(0, ZBLOCK if t < 3 else half)
            lrows = pl.ds(0 if t < 3 else half, ZBLOCK if t < 3 else half)
            rights.append(
                rcopy(pk.at[core, yr, rrows], pk.at[core, yr, rrows], r_send.at[t], r_recv.at[t], right)
            )
            lefts.append(
                rcopy(pk.at[core, yl, lrows], pk.at[core, yl, lrows], l_send.at[t], l_recv.at[t], left)
            )
            rights[t].start()
            lefts[t].start()
        for i, yy in ((0, y),) if t == 0 else ((7, yr),) if t == 4 else ((2 * t - 1, yr), (2 * t, yl)):
            cores.append(core_copy(i, yy))
            cores[-1].start()

    def prompt_part(t, begin, end):
        yr = (y + NY - t) % NY
        yl = (y + t) % NY
        absorb_prompt(q, pk, state, (yr,) if t in (0, 4) else (yr, yl), begin, end)

    def await_cores(t):
        for copy in cores[0:1] if t == 0 else cores[7:8] if t == 4 else cores[2 * t - 1 : 2 * t + 1]:
            copy.wait()

    fetch[2].wait()
    ring_step(0)
    absorb_new(q, kvn, state)
    along_z(0)
    await_cores(0)
    prompt_part(0, 0, 4)
    along_z(1)
    ring_step(1)
    await_cores(1)
    prompt_part(1, 0, 2)
    along_z(2)
    along_y(0)
    prompt_part(1, 2, 4)
    along_z(3)
    ring_step(2)
    await_cores(2)
    prompt_part(2, 0, 2)
    along_y(1)
    prompt_part(2, 2, 4)
    ring_step(3)
    await_cores(3)
    prompt_part(3, 0, 2)
    along_y(2)
    prompt_part(3, 2, 4)
    ring_step(4)
    along_y(3)
    await_cores(4)
    prompt_part(4, 0, 4)
    limit = lens[anc[dom * PG + ctx]]
    outs = []
    for g in range(KVH):
        wait_all(p_copy, g)
        absorb_pages(q, gbuf, limit, state, g)
        finish(state, out, g)
        cols = pl.ds(g * GQ * HD, GQ * HD)
        outs.append(pltpu.make_async_copy(out.at[:, cols], out_hbm.at[:, cols], out_sem.at[g]))
        outs[-1].start()
    for t in range(4):
        rights[t].wait_send()
        lefts[t].wait_send()
    for copy in outs:
        copy.wait()


BLOCK = GQ * SPAN


def queries_of(q, g):
    return jnp.concatenate(
        [q[:, pl.ds(pl.multiple_of(g * BLOCK + j * HD, HD), HD)] for j in range(GQ)], axis=0
    )


def absorb(q, state, g, keys, values, visible, first):
    m_ref, l_ref, acc_ref = state
    n = keys.shape[0]
    scores = lax.dot_general(
        queries_of(q, g), keys, (((1,), (1,)), ((), ())), preferred_element_type=jnp.float32
    )
    if visible is not None:
        scores = jnp.where(visible, scores, NEGATIVE)
    top = scores[:, :HD]
    for i in range(1, n // HD):
        top = jnp.maximum(top, scores[:, i * HD : (i + 1) * HD])
    if not first:
        m_old = m_ref[g]
        top = jnp.maximum(top, m_old)
    m_new = jnp.broadcast_to(jnp.max(top, axis=1, keepdims=True), (BLOCK, HD))
    weights = [jnp.exp2((scores[:, i * HD : (i + 1) * HD] - m_new) * SCALE) for i in range(n // HD)]
    total = weights[0]
    for part in weights[1:]:
        total = total + part
    weights = jnp.concatenate(weights, axis=1)
    added = jnp.dot(weights.astype(jnp.bfloat16), values, preferred_element_type=jnp.float32)
    if first:
        l_ref[g] = total
        acc_ref[g] = added
    else:
        factor = jnp.exp2((m_old - m_new) * SCALE)
        l_ref[g] = factor * l_ref[g] + total
        acc_ref[g] = factor * acc_ref[g] + added
    m_ref[g] = m_new


def head_cols(g):
    return pl.ds(pl.multiple_of(g * HD, HD), HD)


def absorb_new(q, kvn, state):
    def step(g, carry):
        cols = head_cols(g)
        row = lax.broadcasted_iota(jnp.int32, (BLOCK, SPAN), 0) % SPAN
        col = lax.broadcasted_iota(jnp.int32, (BLOCK, SPAN), 1)
        absorb(q, state, g, kvn[0, :, cols], kvn[1, :, cols], col <= row, True)
        return carry

    lax.fori_loop(0, KVH, step, 0)


def absorb_prompt(q, pk, state, blocks, begin, end):
    def step(g, carry):
        cols = head_cols(g)
        keys = jnp.concatenate([pk[0, b, :, cols] for b in blocks], axis=0)
        values = jnp.concatenate([pk[1, b, :, cols] for b in blocks], axis=0)
        absorb(q, state, g, keys, values, None, False)
        return carry

    lax.fori_loop(begin, end, step, 0)


def absorb_pages(q, gbuf, limit, state, g):
    pages = gbuf[g].reshape(NCTX, ROWS, HD).astype(jnp.float32)
    keys = pages[:, :PAGE].reshape(NCTX * PAGE, HD).astype(jnp.bfloat16)
    values = pages[:, PAGE:].reshape(NCTX * PAGE, HD).astype(jnp.bfloat16)
    slot = lax.broadcasted_iota(jnp.int32, (BLOCK, NCTX * PAGE), 1) // PAGE
    page = (slot % NZLO) * NY + slot // NZLO
    absorb(q, state, g, keys, values, page < limit, False)


def finish(state, out, g):
    m_ref, l_ref, acc_ref = state
    result = acc_ref[g] / jnp.sum(l_ref[g], axis=1, keepdims=True)
    result = result.astype(jnp.bfloat16)
    for j in range(GQ):
        out[:, g * BLOCK + j * HD : g * BLOCK + (j + 1) * HD] = result[j * SPAN : (j + 1) * SPAN]


def attend(anc, lengths, prompt, cache, q, kvn):
    vmem = pl.BlockSpec(memory_space=pltpu.VMEM)
    hbm = pl.BlockSpec(memory_space=pltpu.HBM)
    dma = pltpu.SemaphoreType.DMA
    bf16 = jnp.bfloat16
    return pl.pallas_call(
        attend_kernel,
        out_shape=jax.ShapeDtypeStruct((SPAN, H * HD), bf16),
        in_specs=[hbm, hbm, vmem, vmem, hbm, vmem],
        out_specs=hbm,
        scratch_shapes=[
            pltpu.SMEM((PG * NDOM,), jnp.int32),
            pltpu.SMEM((PG * NDOM,), jnp.int32),
            pltpu.VMEM((SPAN, H * HD), bf16),
            pltpu.VMEM((SPAN, H * HD), bf16),
            pltpu.VMEM((2, NY, ZBLOCK, KVW), bf16),
            pltpu.VMEM((KVH, 8, 2, RUN, HD), bf16),
            pltpu.VMEM((KVH, 8, 2, RUN, HD), bf16),
            pltpu.VMEM((KVH, NY, RUN, HD), bf16),
            pltpu.VMEM((KVH, NY, RUN, HD), bf16),
        ]
        + [pltpu.VMEM((KVH, BLOCK, HD), jnp.float32)] * 3
        + [pltpu.VMEM((8, 2, RUN, HD), bf16)] * (2 * KVH)
        + [
            dma((3,)), dma((3,)), dma((3,)), dma((4,)), dma((4,)), dma((4,)), dma((4,)),
            dma((8,)), dma((8,)),
        ]
        + [dma((KVH, 8))] * 6
        + [dma((KVH,))],
        compiler_params=pltpu.CompilerParams(
            collective_id=0, has_side_effects=True, vmem_limit_bytes=50 * 2**20
        ),
        name="attend",
    )(anc, lengths, prompt, cache, q, kvn)


def on_device(q_new, kv_new, prompt_kv, cache_kv, ancestors, lengths):
    prompt = prompt_kv.transpose(1, 0, 2)
    cache = cache_kv.transpose(0, 2, 1, 3).reshape(PG, ROWS, KVW)
    kvn = kv_new.transpose(1, 0, 2)
    return attend(ancestors, lengths, prompt, cache, q_new, kvn)


def solution(mesh):
    placed = (
        P(("dom", "ctx"), None),
        P(("dom", "ctx"), None, None),
        P("ctx", None, None),
        P("dom", "ctx", None, None),
        P(),
        P(),
    )
    return jax.shard_map(
        on_device, mesh=mesh, in_specs=placed, out_specs=P(("dom", "ctx"), None), check_vma=False
    )
```

```python
import functools

import jax
import jax.numpy as jnp
from jax import lax
from jax.experimental import pallas as pl
from jax.experimental.pallas import tpu as pltpu
from jax.sharding import PartitionSpec as P

HD = 128
H = 32
KVH = 4
SPAN = 128
PAGE = 8
GQ = 8
NDOM = 16
NCTX = 32
NY = 8
NZLO = 4
PG = 32
CAP = 4
SHARD = 64
ZBLOCK = SHARD * NZLO
KVW = KVH * HD
ROWS = 2 * PAGE
RUN = CAP * ROWS
FAR_FIRST = (4, 3, 5, 2, 6, 1, 7)
NEGATIVE = -1e30
SCALE = HD ** (-0.5) * 1.4426950408889634


def place():
    dom = lax.axis_index("dom")
    ctx = lax.axis_index("ctx")
    core = dom % 2
    z_hi = (dom // 2) % 2
    x = dom // 4
    z_lo = ctx // NY
    y = ctx % NY
    return dom, ctx, x, z_hi, core, z_lo, y


def at_z(x, core, y, z):
    z = z % (2 * NZLO)
    return {"dom": (x * 2 + z // NZLO) * 2 + core, "ctx": (z % NZLO) * NY + y}


def rcopy(src, dst, send, recv, target):
    return pltpu.make_async_remote_copy(
        src_ref=src,
        dst_ref=dst,
        send_sem=send,
        recv_sem=recv,
        device_id=target,
        device_id_type=pl.DeviceIdType.MESH,
    )


def attend_kernel(
    anc_hbm, len_hbm, prompt_hbm, cache_hbm, q_hbm, kvn_hbm, out_hbm,
    anc, lens, local, cache_raw, cache, prompt, kvn_raw, kvn, q, out, pk, abuf, bbuf, ybuf, gbuf, m_ref, l_ref, acc_ref,
    ar0, ar1, ar2, ar3, br0, br1, br2, br3, in_sem,
    z_send, z_recv, r_send, r_recv, l_send, l_recv, c_send, c_recv,
    a_send, a_recv, b_send, b_recv, p_send, p_recv, out_sem,
):
    dom, ctx, x, z_hi, core, z_lo, y = place()
    z = z_hi * NZLO + z_lo
    e = x * 2 + core
    sibling = {"dom": dom + 1 - 2 * core, "ctx": ctx}
    right = {"dom": dom, "ctx": z_lo * NY + (y + 1) % NY}
    left = {"dom": dom, "ctx": z_lo * NY + (y + NY - 1) % NY}
    state = (m_ref, l_ref, acc_ref)
    arecv, brecv = (ar0, ar1, ar2, ar3), (br0, br1, br2, br3)

    def at_e(o):
        other = (e + o) % NY
        return {"dom": ((other // 2) * 2 + z_hi) * 2 + other % 2, "ctx": ctx}

    def at_y(o):
        return {"dom": dom, "ctx": z_lo * NY + (y + o) % NY}

    barrier = pltpu.get_barrier_semaphore()
    fetch = [
        pltpu.make_async_copy(anc_hbm, anc, in_sem.at[0]),
        pltpu.make_async_copy(prompt_hbm, prompt, in_sem.at[1]),
        pltpu.make_async_copy(cache_hbm, cache_raw, in_sem.at[5]),
        pltpu.make_async_copy(len_hbm, lens, in_sem.at[2]),
        pltpu.make_async_copy(kvn_hbm, kvn_raw, in_sem.at[3]),
        pltpu.make_async_copy(q_hbm, q, in_sem.at[4]),
    ]
    for copy in fetch:
        copy.start()
    for o in range(1, NY):
        for target in (at_e(o), at_z(x, core, y, z + o), at_y(o)):
            pl.semaphore_signal(barrier, inc=1, device_id=target, device_id_type=pl.DeviceIdType.MESH)
    own_rows = pl.ds(z_lo * SHARD, SHARD)
    fetch[1].wait()
    both = jnp.swapaxes(prompt[...], 0, 1)
    pk[core, y, own_rows, :] = jnp.where(core == 0, both[0], both[1])
    pl.semaphore_wait(barrier, 3 * (NY - 1))

    far = 2 - 4 * (z % 2)
    z_copies = [
        rcopy(pk.at[core, y, own_rows], pk.at[core, y, own_rows], z_send.at[i], z_recv.at[i],
              at_z(x, core, y, z + hop + 8))
        for i, hop in enumerate((far, 1, -1))
    ]
    for copy in z_copies:
        copy.start()

    fetch[0].wait()

    def choose(d, carry):
        run = 0
        for r in range(PG // CAP):
            run = jnp.where(anc[d * PG + r * CAP] // PG == dom, r, run)
        for k in range(CAP):
            local[d * CAP + k] = anc[d * PG + run * CAP + k] % PG
        return carry

    lax.fori_loop(0, NDOM, choose, 0, unroll=4)

    def pick_first(g):
        pages = jnp.swapaxes(cache_raw[:, :, :, g * HD : (g + 1) * HD], 1, 2)
        cache[g] = pages.reshape(PG, ROWS, HD)

        def pick(d, carry):
            for k in range(CAP):
                abuf[g, (d // 4) * 2 + d % 2, (d // 2) % 2, k * ROWS : (k + 1) * ROWS, :] = cache[
                    g, local[d * CAP + k]
                ]
            return carry

        lax.fori_loop(0, NDOM, pick, 0, unroll=4)

    fetch[2].wait()
    pick_first(0)
    def a_copy(g, o):
        return rcopy(abuf.at[g, (e + o) % NY], arecv[g].at[e], a_send.at[g, o], a_recv.at[g, o], at_e(o))

    def b_copy(g, o):
        return rcopy(bbuf.at[g, (z + o) % NY], brecv[g].at[z], b_send.at[g, o], b_recv.at[g, o],
                     at_z(x, core, y, z + o))

    def p_copy(g, o):
        return rcopy(ybuf.at[g, (y + o) % NY], gbuf.at[g, y], p_send.at[g, o], p_recv.at[g, o], at_y(o))

    def start_all(make, g):
        for o in FAR_FIRST:
            make(g, o).start()

    def wait_all(make, g):
        for o in FAR_FIRST:
            make(g, o).wait()

    def along_x(g):
        if g > 0:
            pick_first(g)
        start_all(a_copy, g)
        arecv[g][e] = abuf[g, e]

    def along_z(g):
        wait_all(a_copy, g)

        def pick(zz, carry):
            to_hi = zz // NZLO
            for j in range(2):
                source = anc[(x * 4 + to_hi * 2 + core) * PG + (zz % NZLO) * 8 + j * CAP] // PG
                bbuf[g, zz, j] = arecv[g][(source // 4) * 2 + source % 2, to_hi]
            return carry

        lax.fori_loop(0, NY, pick, 0, unroll=4)
        start_all(b_copy, g)
        brecv[g][z] = bbuf[g, z]

    def along_y(g):
        wait_all(b_copy, g)
        for j in range(2):
            source = anc[dom * PG + z_lo * 8 + j * CAP] // PG
            for zl in range(NZLO):
                pages = brecv[g][((source // 2) % 2) * NZLO + zl, j]
                for k in range(CAP):
                    ybuf[g, j * CAP + k, zl * ROWS : (zl + 1) * ROWS, :] = pages[k * ROWS : (k + 1) * ROWS]
        start_all(p_copy, g)
        gbuf[g, y] = ybuf[g, y]

    half = ZBLOCK // 2

    def piece(yy, p):
        return pk.at[core, yy, pl.ds(p * half, half)]

    def hop_copy(t, p, to_right):
        yy = (y + NY - t) % NY if to_right else (y + t) % NY
        send, recv = (r_send, r_recv) if to_right else (l_send, l_recv)
        return rcopy(piece(yy, p), piece(yy, p), send.at[t, p], recv.at[t, p], right if to_right else left)

    def core_copy(t, p, to_right):
        yy = (y + NY - t) % NY if to_right else (y + t) % NY
        i = t if to_right else NY - t
        return rcopy(piece(yy, p), piece(yy, p), c_send.at[i, p], c_recv.at[i, p], sibling)

    def sides(t, p):
        return (True,) if t == 0 or (t == 4 and p == 0) else (False,) if t == 4 else (True, False)

    def ring_step(t, p):
        if t == 0 and p == 0:
            for copy in z_copies:
                copy.wait()
        for side in sides(t, p):
            if t > 0:
                hop_copy(t - 1, p, side).wait_recv()
            if t < 3 or (t == 3 and side == (p == 0)):
                hop_copy(t, p, side).start()
                if t == 0:
                    hop_copy(t, p, False).start()
            core_copy(t, p, side).start()

    def near_part(g, carry):
        absorb_near(q, pk, kvn, state, y, g)
        return carry

    def await_cores(t):
        for p in range(2):
            for side in sides(t, p):
                core_copy(t, p, side).wait()

    along_x(0)
    along_x(1)
    along_x(2)
    along_x(3)
    along_z(0)
    ring_step(0, 0)
    ring_step(0, 1)
    along_z(1)
    for copy in fetch[3:]:
        copy.wait()
    kvn[...] = jnp.swapaxes(kvn_raw[...], 0, 1)
    await_cores(0)
    lax.fori_loop(0, KVH, near_part, 0)
    along_z(2)
    ring_step(1, 0)
    ring_step(1, 1)
    along_z(3)
    await_cores(1)

    def ring_part(i, carry):
        @pl.when(i == 1)
        def _():
            along_y(0)

        @pl.when(i == 4)
        def _():
            ring_step(2, 0)
            ring_step(2, 1)
            await_cores(2)

        @pl.when(i == 5)
        def _():
            along_y(1)

        @pl.when(i == 8)
        def _():
            ring_step(3, 0)
            ring_step(3, 1)
            await_cores(3)

        @pl.when(i == 9)
        def _():
            along_y(2)

        @pl.when(i == 11)
        def _():
            along_y(3)

        absorb_ring(q, pk, state, y, 1 + i // KVH, i % KVH)
        return carry

    lax.fori_loop(0, 3 * KVH, ring_part, 0)
    ring_step(4, 0)
    ring_step(4, 1)
    await_cores(4)
    limit = lens[anc[dom * PG + ctx]]

    def out_copy(g):
        cols = pl.ds(pl.multiple_of(g * BLOCK, BLOCK), BLOCK)
        return pltpu.make_async_copy(out.at[:, cols], out_hbm.at[:, cols], out_sem.at[g])

    def last_part(g, carry):
        wait_all(p_copy, g)
        absorb_last(q, pk, gbuf, limit, state, y, g)
        finish(state, out, g)
        out_copy(g).start()
        return carry

    lax.fori_loop(0, KVH, last_part, 0)
    for t in range(4):
        for p in range(2):
            for side in (True, False):
                if t < 3 or side == (p == 0):
                    hop_copy(t, p, side).wait_send()
    for g in range(KVH):
        out_copy(g).wait()


BLOCK = GQ * SPAN


def queries_of(q, g):
    return jnp.concatenate(
        [q[:, pl.ds(pl.multiple_of(g * BLOCK + j * HD, HD), HD)] for j in range(GQ)], axis=0
    )


def absorb(q, state, g, keys, values, masks, first):
    m_ref, l_ref, acc_ref = state
    scores = lax.dot_general(
        queries_of(q, g), keys, (((1,), (1,)), ((), ())), preferred_element_type=jnp.float32
    )
    tiles = [scores[:, i * HD : (i + 1) * HD] for i in range(keys.shape[0] // HD)]
    for i, visible in masks:
        tiles[i] = jnp.where(visible, tiles[i], NEGATIVE)
    top = functools.reduce(jnp.maximum, tiles)
    if not first:
        m_old = m_ref[g]
        top = jnp.maximum(top, m_old)
    m_new = jnp.broadcast_to(jnp.max(top, axis=1, keepdims=True), (BLOCK, HD))
    weights = [jnp.exp2((tile - m_new) * SCALE) for tile in tiles]
    total = functools.reduce(jnp.add, weights)
    weights = jnp.concatenate(weights, axis=1)
    added = jnp.dot(weights.astype(jnp.bfloat16), values, preferred_element_type=jnp.float32)
    if first:
        l_ref[g] = total
        acc_ref[g] = added
    else:
        factor = jnp.exp2((m_old - m_new) * SCALE)
        l_ref[g] = factor * l_ref[g] + total
        acc_ref[g] = factor * acc_ref[g] + added
    m_ref[g] = m_new


def head_cols(g):
    return pl.ds(pl.multiple_of(g * HD, HD), HD)


def absorb_near(q, pk, kvn, state, y, g):
    cols = head_cols(g)
    row = lax.broadcasted_iota(jnp.int32, (BLOCK, SPAN), 0) % SPAN
    col = lax.broadcasted_iota(jnp.int32, (BLOCK, SPAN), 1)
    keys = jnp.concatenate([pk[0, y, :, cols], kvn[0, :, cols]], axis=0)
    values = jnp.concatenate([pk[1, y, :, cols], kvn[1, :, cols]], axis=0)
    absorb(q, state, g, keys, values, [(ZBLOCK // HD, col <= row)], True)


def absorb_ring(q, pk, state, y, t, g):
    cols = head_cols(g)
    blocks = ((y + NY - t) % NY, (y + t) % NY)
    keys = jnp.concatenate([pk[0, b, :, cols] for b in blocks], axis=0)
    values = jnp.concatenate([pk[1, b, :, cols] for b in blocks], axis=0)
    absorb(q, state, g, keys, values, [], False)


def absorb_last(q, pk, gbuf, limit, state, y, g):
    cols = head_cols(g)
    far = (y + NY // 2) % NY
    pages = gbuf[g].reshape(NCTX, ROWS, HD).astype(jnp.float32)
    page_keys = pages[:, :PAGE].reshape(NCTX * PAGE, HD).astype(jnp.bfloat16)
    page_values = pages[:, PAGE:].reshape(NCTX * PAGE, HD).astype(jnp.bfloat16)
    keys = jnp.concatenate([pk[0, far, :, cols], page_keys], axis=0)
    values = jnp.concatenate([pk[1, far, :, cols], page_values], axis=0)
    masks = []
    for i in range(NCTX * PAGE // HD):
        slot = (lax.broadcasted_iota(jnp.int32, (BLOCK, HD), 1) + i * HD) // PAGE
        page = (slot % NZLO) * NY + slot // NZLO
        masks.append((ZBLOCK // HD + i, page < limit))
    absorb(q, state, g, keys, values, masks, False)


def finish(state, out, g):
    m_ref, l_ref, acc_ref = state
    result = acc_ref[g] / jnp.sum(l_ref[g], axis=1, keepdims=True)
    result = result.astype(jnp.bfloat16)
    for j in range(GQ):
        out[:, pl.ds(pl.multiple_of(g * BLOCK + j * HD, HD), HD)] = result[j * SPAN : (j + 1) * SPAN]


def attend(anc, lengths, prompt, cache, q, kvn):
    hbm = pl.BlockSpec(memory_space=pltpu.HBM)
    dma = pltpu.SemaphoreType.DMA
    bf16 = jnp.bfloat16
    return pl.pallas_call(
        attend_kernel,
        out_shape=jax.ShapeDtypeStruct((SPAN, H * HD), bf16),
        in_specs=[hbm] * 6,
        out_specs=hbm,
        scratch_shapes=[
            pltpu.SMEM((PG * NDOM,), jnp.int32),
            pltpu.SMEM((PG * NDOM,), jnp.int32),
            pltpu.SMEM((CAP * NDOM,), jnp.int32),
            pltpu.VMEM((PG, PAGE, 2, KVW), bf16),
            pltpu.VMEM((KVH, PG, ROWS, HD), bf16),
            pltpu.VMEM((SHARD, 2, KVW), bf16),
            pltpu.VMEM((SPAN, 2, KVW), bf16),
            pltpu.VMEM((2, SPAN, KVW), bf16),
            pltpu.VMEM((SPAN, H * HD), bf16),
            pltpu.VMEM((SPAN, H * HD), bf16),
            pltpu.VMEM((2, NY, ZBLOCK, KVW), bf16),
            pltpu.VMEM((KVH, 8, 2, RUN, HD), bf16),
            pltpu.VMEM((KVH, 8, 2, RUN, HD), bf16),
            pltpu.VMEM((KVH, NY, RUN, HD), bf16),
            pltpu.VMEM((KVH, NY, RUN, HD), bf16),
        ]
        + [pltpu.VMEM((KVH, BLOCK, HD), jnp.float32)] * 3
        + [pltpu.VMEM((8, 2, RUN, HD), bf16)] * (2 * KVH)
        + [
            dma((6,)), dma((3,)), dma((3,)), dma((4, 2)), dma((4, 2)), dma((4, 2)), dma((4, 2)),
            dma((8, 2)), dma((8, 2)),
        ]
        + [dma((KVH, 8))] * 6
        + [dma((KVH,))],
        compiler_params=pltpu.CompilerParams(
            collective_id=0, has_side_effects=True, vmem_limit_bytes=50 * 2**20
        ),
        name="attend",
    )(anc, lengths, prompt, cache, q, kvn)


def on_device(q_new, kv_new, prompt_kv, cache_kv, ancestors, lengths):
    args = (ancestors, lengths, prompt_kv, cache_kv, q_new, kv_new)
    return attend(*[pltpu.with_memory_space_constraint(a, pltpu.HBM) for a in args])


def solution(mesh):
    placed = (
        P(("dom", "ctx"), None),
        P(("dom", "ctx"), None, None),
        P("ctx", None, None),
        P("dom", "ctx", None, None),
        P(),
        P(),
    )
    return jax.shard_map(
        on_device, mesh=mesh, in_specs=placed, out_specs=P(("dom", "ctx"), None), check_vma=False
    )
```

```python
import functools

import jax
import jax.numpy as jnp
from jax import lax
from jax.experimental import pallas as pl
from jax.experimental.pallas import tpu as pltpu
from jax.sharding import PartitionSpec as P

HD = 128
H = 32
KVH = 4
SPAN = 128
PAGE = 8
GQ = 8
NDOM = 16
NCTX = 32
NY = 8
NZLO = 4
PG = 32
CAP = 4
SHARD = 64
ZBLOCK = SHARD * NZLO
KVW = KVH * HD
ROWS = 2 * PAGE
RUN = CAP * ROWS
FAR_FIRST = (4, 3, 5, 2, 6, 1, 7)
NEGATIVE = -1e30
SCALE = HD ** (-0.5) * 1.4426950408889634


def place():
    dom = lax.axis_index("dom")
    ctx = lax.axis_index("ctx")
    core = dom % 2
    z_hi = (dom // 2) % 2
    x = dom // 4
    z_lo = ctx // NY
    y = ctx % NY
    return dom, ctx, x, z_hi, core, z_lo, y


def at_z(x, core, y, z):
    z = z % (2 * NZLO)
    return {"dom": (x * 2 + z // NZLO) * 2 + core, "ctx": (z % NZLO) * NY + y}


def rcopy(src, dst, send, recv, target):
    return pltpu.make_async_remote_copy(
        src_ref=src,
        dst_ref=dst,
        send_sem=send,
        recv_sem=recv,
        device_id=target,
        device_id_type=pl.DeviceIdType.MESH,
    )


def attend_kernel(
    anc_hbm, len_hbm, prompt_hbm, cache_hbm, q_hbm, kvn_hbm, out_hbm,
    anc, lens, local, cache_raw, cache, prompt, kvn_raw, kvn, q, out, pk, abuf, bbuf, ybuf, gbuf, m_ref, l_ref, acc_ref,
    ar0, ar1, ar2, ar3, br0, br1, br2, br3, in_sem,
    z_send, z_recv, r_send, r_recv, l_send, l_recv, c_send, c_recv,
    a_send, a_recv, b_send, b_recv, p_send, p_recv, out_sem,
):
    dom, ctx, x, z_hi, core, z_lo, y = place()
    z = z_hi * NZLO + z_lo
    e = x * 2 + core
    sibling = {"dom": dom + 1 - 2 * core, "ctx": ctx}
    right = {"dom": dom, "ctx": z_lo * NY + (y + 1) % NY}
    left = {"dom": dom, "ctx": z_lo * NY + (y + NY - 1) % NY}
    state = (m_ref, l_ref, acc_ref)
    arecv, brecv = (ar0, ar1, ar2, ar3), (br0, br1, br2, br3)

    def at_e(o):
        other = (e + o) % NY
        return {"dom": ((other // 2) * 2 + z_hi) * 2 + other % 2, "ctx": ctx}

    def at_y(o):
        return {"dom": dom, "ctx": z_lo * NY + (y + o) % NY}

    barrier = pltpu.get_barrier_semaphore()
    fetch = [
        pltpu.make_async_copy(anc_hbm, anc, in_sem.at[0]),
        pltpu.make_async_copy(prompt_hbm, prompt, in_sem.at[1]),
        pltpu.make_async_copy(cache_hbm, cache_raw, in_sem.at[5]),
        pltpu.make_async_copy(len_hbm, lens, in_sem.at[2]),
        pltpu.make_async_copy(kvn_hbm, kvn_raw, in_sem.at[3]),
        pltpu.make_async_copy(q_hbm, q, in_sem.at[4]),
    ]
    for copy in fetch:
        copy.start()
    for o in range(1, NY):
        for target in (at_e(o), at_z(x, core, y, z + o), at_y(o)):
            pl.semaphore_signal(barrier, inc=1, device_id=target, device_id_type=pl.DeviceIdType.MESH)
    own_rows = pl.ds(z_lo * SHARD, SHARD)
    fetch[1].wait()
    both = jnp.swapaxes(prompt[...], 0, 1)
    pk[core, y, own_rows, :] = jnp.where(core == 0, both[0], both[1])
    pl.semaphore_wait(barrier, 3 * (NY - 1))

    far = 2 - 4 * (z % 2)
    z_copies = [
        rcopy(pk.at[core, y, own_rows], pk.at[core, y, own_rows], z_send.at[i], z_recv.at[i],
              at_z(x, core, y, z + hop + 8))
        for i, hop in enumerate((far, 1, -1))
    ]
    for copy in z_copies:
        copy.start()

    fetch[0].wait()

    def choose(d, carry):
        run = 0
        for r in range(PG // CAP):
            run = jnp.where(anc[d * PG + r * CAP] // PG == dom, r, run)
        for k in range(CAP):
            local[d * CAP + k] = anc[d * PG + run * CAP + k] % PG
        return carry

    lax.fori_loop(0, NDOM, choose, 0, unroll=4)

    def pick_first(g):
        pages = jnp.swapaxes(cache_raw[:, :, :, g * HD : (g + 1) * HD], 1, 2)
        cache[g] = pages.reshape(PG, ROWS, HD)

        def pick(d, carry):
            for k in range(CAP):
                abuf[g, (d // 4) * 2 + d % 2, (d // 2) % 2, k * ROWS : (k + 1) * ROWS, :] = cache[
                    g, local[d * CAP + k]
                ]
            return carry

        lax.fori_loop(0, NDOM, pick, 0, unroll=4)

    fetch[2].wait()
    pick_first(0)
    def a_copy(g, o):
        return rcopy(abuf.at[g, (e + o) % NY], arecv[g].at[e], a_send.at[g, o], a_recv.at[g, o], at_e(o))

    def b_copy(g, o):
        return rcopy(bbuf.at[g, (z + o) % NY], brecv[g].at[z], b_send.at[g, o], b_recv.at[g, o],
                     at_z(x, core, y, z + o))

    def p_copy(g, o):
        return rcopy(ybuf.at[g, (y + o) % NY], gbuf.at[g, y], p_send.at[g, o], p_recv.at[g, o], at_y(o))

    def start_all(make, g):
        for o in FAR_FIRST:
            make(g, o).start()

    def wait_all(make, g):
        for o in FAR_FIRST:
            make(g, o).wait()

    def along_x(g):
        if g > 0:
            pick_first(g)
        start_all(a_copy, g)
        arecv[g][e] = abuf[g, e]

    def along_z(g):
        wait_all(a_copy, g)

        def pick(zz, carry):
            to_hi = zz // NZLO
            for j in range(2):
                source = anc[(x * 4 + to_hi * 2 + core) * PG + (zz % NZLO) * 8 + j * CAP] // PG
                bbuf[g, zz, j] = arecv[g][(source // 4) * 2 + source % 2, to_hi]
            return carry

        lax.fori_loop(0, NY, pick, 0, unroll=4)
        start_all(b_copy, g)
        brecv[g][z] = bbuf[g, z]

    def along_y(g):
        wait_all(b_copy, g)
        for j in range(2):
            source = anc[dom * PG + z_lo * 8 + j * CAP] // PG
            for zl in range(NZLO):
                pages = brecv[g][((source // 2) % 2) * NZLO + zl, j]
                for k in range(CAP):
                    ybuf[g, j * CAP + k, zl * ROWS : (zl + 1) * ROWS, :] = pages[k * ROWS : (k + 1) * ROWS]
        start_all(p_copy, g)
        gbuf[g, y] = ybuf[g, y]

    half = ZBLOCK // 2

    def piece(yy, p):
        return pk.at[core, yy, pl.ds(p * half, half)]

    def hop_copy(t, p, to_right):
        yy = (y + NY - t) % NY if to_right else (y + t) % NY
        send, recv = (r_send, r_recv) if to_right else (l_send, l_recv)
        return rcopy(piece(yy, p), piece(yy, p), send.at[t, p], recv.at[t, p], right if to_right else left)

    def core_copy(t, p, to_right):
        yy = (y + NY - t) % NY if to_right else (y + t) % NY
        i = t if to_right else NY - t
        return rcopy(piece(yy, p), piece(yy, p), c_send.at[i, p], c_recv.at[i, p], sibling)

    def sides(t, p):
        return (True,) if t == 0 or (t == 4 and p == 0) else (False,) if t == 4 else (True, False)

    def ring_step(t, p):
        if t == 0 and p == 0:
            for copy in z_copies:
                copy.wait()
        for side in sides(t, p):
            if t > 0:
                hop_copy(t - 1, p, side).wait_recv()
            if t < 3 or (t == 3 and side == (p == 0)):
                hop_copy(t, p, side).start()
                if t == 0:
                    hop_copy(t, p, False).start()
            core_copy(t, p, side).start()

    def near_part(g, carry):
        absorb_near(q, pk, kvn, state, y, g)
        return carry

    def await_cores(t):
        for p in range(2):
            for side in sides(t, p):
                core_copy(t, p, side).wait()

    along_x(0)
    along_x(1)
    along_x(2)
    along_x(3)
    along_z(0)
    ring_step(0, 0)
    ring_step(0, 1)
    along_z(1)
    for copy in fetch[3:]:
        copy.wait()
    kvn[...] = jnp.swapaxes(kvn_raw[...], 0, 1)
    await_cores(0)
    lax.fori_loop(0, KVH, near_part, 0)
    along_z(2)
    ring_step(1, 0)
    ring_step(1, 1)
    along_z(3)
    await_cores(1)

    def ring_part(i, carry):
        @pl.when(i == 1)
        def _():
            along_y(0)

        @pl.when(i == 4)
        def _():
            ring_step(2, 0)
            ring_step(2, 1)
            await_cores(2)

        @pl.when(i == 5)
        def _():
            along_y(1)

        @pl.when(i == 8)
        def _():
            ring_step(3, 0)
            ring_step(3, 1)
            await_cores(3)

        @pl.when(i == 9)
        def _():
            along_y(2)

        @pl.when(i == 11)
        def _():
            ring_step(4, 0)
            ring_step(4, 1)
            along_y(3)

        absorb_ring(q, pk, state, y, 1 + i // KVH, i % KVH)
        return carry

    lax.fori_loop(0, 3 * KVH, ring_part, 0)
    await_cores(4)
    limit = lens[anc[dom * PG + ctx]]

    def out_copy(g):
        cols = pl.ds(pl.multiple_of(g * BLOCK, BLOCK), BLOCK)
        return pltpu.make_async_copy(out.at[:, cols], out_hbm.at[:, cols], out_sem.at[g])

    def last_part(g, carry):
        wait_all(p_copy, g)
        absorb_last(q, pk, gbuf, limit, state, y, g)
        finish(state, out, g)
        out_copy(g).start()
        return carry

    lax.fori_loop(0, KVH, last_part, 0)
    for t in range(4):
        for p in range(2):
            for side in (True, False):
                if t < 3 or side == (p == 0):
                    hop_copy(t, p, side).wait_send()
    for g in range(KVH):
        out_copy(g).wait()


BLOCK = GQ * SPAN


def queries_of(q, g):
    return jnp.concatenate(
        [q[:, pl.ds(pl.multiple_of(g * BLOCK + j * HD, HD), HD)] for j in range(GQ)], axis=0
    )


def absorb(q, state, g, keys, values, masks, first):
    m_ref, l_ref, acc_ref = state
    scores = lax.dot_general(
        queries_of(q, g), keys, (((1,), (1,)), ((), ())), preferred_element_type=jnp.float32
    )
    tiles = [scores[:, i * HD : (i + 1) * HD] for i in range(keys.shape[0] // HD)]
    for i, visible in masks:
        tiles[i] = jnp.where(visible, tiles[i], NEGATIVE)
    top = functools.reduce(jnp.maximum, tiles)
    if not first:
        m_old = m_ref[g]
        top = jnp.maximum(top, m_old)
    m_new = jnp.broadcast_to(jnp.max(top, axis=1, keepdims=True), (BLOCK, HD))
    weights = [jnp.exp2((tile - m_new) * SCALE) for tile in tiles]
    total = functools.reduce(jnp.add, weights)
    weights = jnp.concatenate(weights, axis=1)
    added = jnp.dot(weights.astype(jnp.bfloat16), values, preferred_element_type=jnp.float32)
    if first:
        l_ref[g] = total
        acc_ref[g] = added
    else:
        factor = jnp.exp2((m_old - m_new) * SCALE)
        l_ref[g] = factor * l_ref[g] + total
        acc_ref[g] = factor * acc_ref[g] + added
    m_ref[g] = m_new


def head_cols(g):
    return pl.ds(pl.multiple_of(g * HD, HD), HD)


def absorb_near(q, pk, kvn, state, y, g):
    cols = head_cols(g)
    row = lax.broadcasted_iota(jnp.int32, (BLOCK, SPAN), 0) % SPAN
    col = lax.broadcasted_iota(jnp.int32, (BLOCK, SPAN), 1)
    keys = jnp.concatenate([pk[0, y, :, cols], kvn[0, :, cols]], axis=0)
    values = jnp.concatenate([pk[1, y, :, cols], kvn[1, :, cols]], axis=0)
    absorb(q, state, g, keys, values, [(ZBLOCK // HD, col <= row)], True)


def absorb_ring(q, pk, state, y, t, g):
    cols = head_cols(g)
    blocks = ((y + NY - t) % NY, (y + t) % NY)
    keys = jnp.concatenate([pk[0, b, :, cols] for b in blocks], axis=0)
    values = jnp.concatenate([pk[1, b, :, cols] for b in blocks], axis=0)
    absorb(q, state, g, keys, values, [], False)


def absorb_last(q, pk, gbuf, limit, state, y, g):
    cols = head_cols(g)
    far = (y + NY // 2) % NY
    pages = gbuf[g].reshape(NCTX, ROWS, HD).astype(jnp.float32)
    page_keys = pages[:, :PAGE].reshape(NCTX * PAGE, HD).astype(jnp.bfloat16)
    page_values = pages[:, PAGE:].reshape(NCTX * PAGE, HD).astype(jnp.bfloat16)
    keys = jnp.concatenate([pk[0, far, :, cols], page_keys], axis=0)
    values = jnp.concatenate([pk[1, far, :, cols], page_values], axis=0)
    masks = []
    for i in range(NCTX * PAGE // HD):
        slot = (lax.broadcasted_iota(jnp.int32, (BLOCK, HD), 1) + i * HD) // PAGE
        page = (slot % NZLO) * NY + slot // NZLO
        masks.append((ZBLOCK // HD + i, page < limit))
    absorb(q, state, g, keys, values, masks, False)


def finish(state, out, g):
    m_ref, l_ref, acc_ref = state
    result = acc_ref[g] / jnp.sum(l_ref[g], axis=1, keepdims=True)
    result = result.astype(jnp.bfloat16)
    for j in range(GQ):
        out[:, pl.ds(pl.multiple_of(g * BLOCK + j * HD, HD), HD)] = result[j * SPAN : (j + 1) * SPAN]


def attend(anc, lengths, prompt, cache, q, kvn):
    hbm = pl.BlockSpec(memory_space=pltpu.HBM)
    dma = pltpu.SemaphoreType.DMA
    bf16 = jnp.bfloat16
    return pl.pallas_call(
        attend_kernel,
        out_shape=jax.ShapeDtypeStruct((SPAN, H * HD), bf16),
        in_specs=[hbm] * 6,
        out_specs=hbm,
        scratch_shapes=[
            pltpu.SMEM((PG * NDOM,), jnp.int32),
            pltpu.SMEM((PG * NDOM,), jnp.int32),
            pltpu.SMEM((CAP * NDOM,), jnp.int32),
            pltpu.VMEM((PG, PAGE, 2, KVW), bf16),
            pltpu.VMEM((KVH, PG, ROWS, HD), bf16),
            pltpu.VMEM((SHARD, 2, KVW), bf16),
            pltpu.VMEM((SPAN, 2, KVW), bf16),
            pltpu.VMEM((2, SPAN, KVW), bf16),
            pltpu.VMEM((SPAN, H * HD), bf16),
            pltpu.VMEM((SPAN, H * HD), bf16),
            pltpu.VMEM((2, NY, ZBLOCK, KVW), bf16),
            pltpu.VMEM((KVH, 8, 2, RUN, HD), bf16),
            pltpu.VMEM((KVH, 8, 2, RUN, HD), bf16),
            pltpu.VMEM((KVH, NY, RUN, HD), bf16),
            pltpu.VMEM((KVH, NY, RUN, HD), bf16),
        ]
        + [pltpu.VMEM((KVH, BLOCK, HD), jnp.float32)] * 3
        + [pltpu.VMEM((8, 2, RUN, HD), bf16)] * (2 * KVH)
        + [
            dma((6,)), dma((3,)), dma((3,)), dma((4, 2)), dma((4, 2)), dma((4, 2)), dma((4, 2)),
            dma((8, 2)), dma((8, 2)),
        ]
        + [dma((KVH, 8))] * 6
        + [dma((KVH,))],
        compiler_params=pltpu.CompilerParams(
            collective_id=0, has_side_effects=True, vmem_limit_bytes=50 * 2**20
        ),
        name="attend",
    )(anc, lengths, prompt, cache, q, kvn)


def on_device(q_new, kv_new, prompt_kv, cache_kv, ancestors, lengths):
    args = (ancestors, lengths, prompt_kv, cache_kv, q_new, kv_new)
    return attend(*[pltpu.with_memory_space_constraint(a, pltpu.HBM) for a in args])


def solution(mesh):
    placed = (
        P(("dom", "ctx"), None),
        P(("dom", "ctx"), None, None),
        P("ctx", None, None),
        P("dom", "ctx", None, None),
        P(),
        P(),
    )
    return jax.shard_map(
        on_device, mesh=mesh, in_specs=placed, out_specs=P(("dom", "ctx"), None), check_vma=False
    )
```
